512 devices in a mesh: rep: 8 (over x, core), ep: 64 (over z, y).
Axes of the slice: x: 4, y: 8, z: 8, core: 2. Of those that a mesh axis runs over, the one named last changes fastest.
Arguments:
- tokens: bfloat16 [65536, 1024], P(('rep', 'ep')), may hold values from -6 to 6
- query: bfloat16 [65536, 1024], P(('rep', 'ep')), may hold values from -6 to 6
- expert_ids: int32 [65536, 6], P(('rep', 'ep')), may hold values from 0 to 63, all different within a row; in each aligned block of 128 rows (0 to 127, 128 to 255, ...) at most 13 rows name the same one
- gate_probs: bfloat16 [65536, 6], P(('rep', 'ep')), may hold values from 0.049804688 to 0.34960938
- w_gate_up: bfloat16 [64, 1024, 1408], P('ep'), may hold values from -0.1875 to 0.1875
- w_down: bfloat16 [64, 1024, 704], P('ep', 'rep'), may hold values from -0.1875 to 0.1875
- dir_gate: bfloat16 [64, 1024, 704], P('ep', 'rep'), may hold values from -0.1875 to 0.1875
Outputs:
- hvp_gate_up: float32 [64, 1024, 1408], P('ep', 'rep')
The draws below stay inside these ranges and needn't reach their ends.
Inputs may be any that keep to these rules, and one draw needn't show every extreme that they name: `expert_ids`: each row names 6 different experts; among the rows of one device no expert is named by more than 13 pairs, and in every draw some expert is named by exactly 13 pairs of some device.
All inputs are finite; a program needn't handle non-finite values.
Results may differ from the reference program's by a relative error of at most 0.015.
Values may be sent and summed in bfloat16 or wider, within the bound.
No kernel may reach another device: no remote copies, remote signals or barrier semaphores. Data moves between devices by JAX's collectives and lax.ppermute only.
A program may use at most 64 MiB of HBM per device.

```python
import math
import jax
import jax.numpy as jnp
import numpy as np
from jax import lax

D = 1024
FF = 704
TOPK = 6
TOK_DEV = 128
EXPERTS = 64
CAP = 13
TOK_REP = 8192
TOKENS = 65536
N_REP = 8
N_EP = 64


def levels(stream_key, shape, pieces, smallest, largest):
    level, own = 1.0, jax.random.fold_in(stream_key, 6)
    for axis_at, blocks in pieces:
        steps = jnp.exp(jax.random.uniform(jax.random.fold_in(own, axis_at), (blocks,), jnp.float32, smallest / len(pieces), largest / len(pieces)))
        level = level * jnp.repeat(steps, shape[axis_at] // blocks).reshape([-1 if axis == axis_at else 1 for axis in range(len(shape))])
    return level


def deal_out(rng, own, number, rows, amount, top, reach, skew):
    order = jax.random.permutation(rng, amount)
    crowded, ordinary = shares(amount, rows * top, reach, skew, True), shares(amount, rows * top, reach, skew, False)
    places = jnp.arange(amount)

    def named(lengths, offset_by):
        used = int((lengths > 0).sum())
        fixed = max(1, used // 4)
        moved = fixed + (places - fixed + offset_by * (used - fixed)) % max(1, amount - fixed)
        return jnp.zeros((amount,), jnp.int32).at[order[jnp.where(places < fixed, places, moved)]].set(jnp.asarray(lengths, jnp.int32))

    lengths = jnp.where(number % 4 == 0, named(crowded, number // 4), named(ordinary, number - number // 4 - 1))
    mixed = jax.random.permutation(jax.random.fold_in(own, 3), amount)
    source_of, sink = mixed[0:amount // 2 * 2:2], mixed[1:amount // 2 * 2:2]
    slack = jnp.minimum(lengths[source_of] - 1, reach - lengths[sink]) // 2
    slack = jnp.where((source_of == order[0]) | (sink == order[0]) | (lengths[sink] == 0), 0, jnp.maximum(slack, 0))
    moved = jax.random.randint(jax.random.fold_in(own, 4), (amount // 2,), 0, 1 << 20) % (slack + 1)
    lengths = lengths.at[source_of].add(-moved).at[sink].add(moved)
    items = jnp.searchsorted(jnp.cumsum(lengths), jnp.arange(rows * top), side="right").astype(jnp.int32)
    listing = items.reshape(top, rows).T
    listing = listing[jax.random.permutation(jax.random.fold_in(own, 1), rows)]
    offset_by = jax.random.randint(jax.random.fold_in(own, 2), (rows, 1), 0, top)
    return jnp.take_along_axis(listing, (jnp.arange(top)[None, :] + offset_by) % top, axis=1)


def shares(count, total, most, skew, full):
    loads = [(1 << 20) // math.isqrt(standing ** skew) + 1 for standing in range(1, count + 1)]
    largest = most if full else min(most, max(-(-total // count), total * loads[0] // sum(loads)))
    least = 1 if total - largest >= count - 1 else 0
    counts, spare = [largest] + [least] * (count - 1), total - largest - least * (count - 1)
    while spare > 0:
        movable = [i for i in range(1, count) if counts[i] < largest] or [i for i in range(1, count) if counts[i] < most]
        pool, remaining = sum([loads[i] for i in movable]), spare
        for i in movable:
            extra = min(most - counts[i], max(1, remaining * loads[i] // pool), spare)
            counts[i] = counts[i] + extra
            spare = spare - extra
    return np.array(counts)


def gaussian(key, shape, width, reach, split=(), kind=jnp.bfloat16):
    level = levels(key, shape, split, -0.22, 0.18) if split else 1.0
    result = jax.random.normal(key, shape, jnp.float32) * width * level
    return jnp.minimum(jnp.maximum(result, -reach), reach).astype(kind)


def setup_inputs(seed: int = 0) -> dict:
    arg_keys = jax.random.split(jax.random.key(seed), 8)
    tokens = gaussian(arg_keys[0], (TOKENS, D), 1.0, 6.0, ((0, 512),))
    query = gaussian(arg_keys[1], (TOKENS, D), 1.0, 6.0, ((0, 512),))
    expert_ids_keys = jax.random.split(jax.random.fold_in(arg_keys[2], 1), TOKENS // TOK_DEV)
    expert_ids_turns = jax.random.permutation(jax.random.fold_in(arg_keys[2], 3), TOKENS // TOK_DEV)
    expert_ids = jax.vmap(lambda own, number: deal_out(jax.random.fold_in(arg_keys[2], 2), own, number, TOK_DEV, EXPERTS, TOPK, CAP, 2))(expert_ids_keys, expert_ids_turns).reshape((TOKENS, TOPK))
    gate_probs = jnp.clip(0.049804688 + 0.2998047 * jax.random.uniform(arg_keys[3], (TOKENS, TOPK), jnp.float32) ** levels(arg_keys[3], (TOKENS, TOPK), ((0, 512),), -0.2, 0.2), 0.049804688, 0.34960938).astype(jnp.bfloat16)
    w_gate_up = gaussian(arg_keys[4], (EXPERTS, D, 2 * FF), D ** -0.5, 0.1875, ((0, 64),))
    w_down = gaussian(arg_keys[5], (EXPERTS, D, FF), D ** -0.5, 0.1875, ((0, 64), (1, 8)))
    dir_gate = gaussian(arg_keys[6], (EXPERTS, D, FF), D ** -0.5, 0.1875, ((0, 64), (1, 8)))
    return {"tokens": tokens, "query": query, "expert_ids": expert_ids, "gate_probs": gate_probs, "w_gate_up": w_gate_up, "w_down": w_down, "dir_gate": dir_gate}


def expert_term(token_rows, query_rows, gate_rows, gate_up, down_rows, direction):
    scaled = (gate_rows[:, None].astype(jnp.float32) * query_rows.astype(jnp.float32)).astype(jnp.bfloat16)
    pre_act = jnp.dot(token_rows, gate_up, preferred_element_type=jnp.float32)
    gate_pre = pre_act[:, :FF]
    up_pre = pre_act[:, FF:]
    tangent = jnp.dot(token_rows, direction, preferred_element_type=jnp.float32)
    error_hidden = jnp.dot(scaled, down_rows, preferred_element_type=jnp.float32)
    sigmoid_a = 1.0 / (1.0 + jnp.exp(-gate_pre))
    slope = sigmoid_a * (1.0 + gate_pre * (1.0 - sigmoid_a))
    bend = sigmoid_a * (1.0 - sigmoid_a) * (2.0 + gate_pre * (1.0 - 2.0 * sigmoid_a))
    factors = jnp.concatenate([error_hidden * up_pre * bend * tangent, error_hidden * slope * tangent], axis=1).astype(jnp.bfloat16)
    return jnp.dot(token_rows.T, factors, preferred_element_type=jnp.float32)


def reference(tokens, query, expert_ids, gate_probs, w_gate_up, w_down, dir_gate):
    group_tokens = tokens.reshape(N_REP, TOK_REP, D)
    group_query = query.reshape(N_REP, TOK_REP, D)
    group_ids = expert_ids.reshape(N_REP, TOK_REP, TOPK)
    group_gates = gate_probs.reshape(N_REP, TOK_REP, TOPK)
    limit = N_EP * CAP

    def per_expert(inputs):
        expert, gate_up, down_rows, direction = inputs

        def per_group(group):
            token_block, query_block, id_block, gate_block = group
            routed = id_block == expert
            gate_sum = jnp.sum(jnp.where(routed, gate_block.astype(jnp.float32), jnp.float32(0.0)), axis=1)
            any_routed = jnp.any(routed, axis=1)
            picked = jnp.nonzero(any_routed, size=limit, fill_value=0)[0].astype(jnp.int32)
            total = jnp.sum(any_routed.astype(jnp.int32))
            is_real = jnp.arange(limit, dtype=jnp.int32) < total
            gate_rows = jnp.where(is_real, gate_sum[picked], jnp.float32(0.0)).astype(jnp.bfloat16)
            term = expert_term(token_block[picked], query_block[picked], gate_rows, gate_up, down_rows, direction)
            return term.astype(jnp.bfloat16)

        partials = lax.map(per_group, (group_tokens, group_query, group_ids, group_gates))
        return jnp.sum(partials.astype(jnp.float32), axis=0)

    numbers = jnp.arange(EXPERTS, dtype=jnp.int32)
    return lax.map(per_expert, (numbers, w_gate_up, w_down, dir_gate))
```

```python
import functools

import jax
import jax.numpy as jnp
from jax import lax
from jax.experimental import pallas as pl
from jax.experimental.pallas import tpu as pltpu
from jax.sharding import PartitionSpec as P

F32 = jnp.float32
BF16 = jnp.bfloat16
LANES = 128
GROUP = 8


def dot(a, b, contract=((1,), (0,))):
    return lax.dot_general(a, b, (contract, ((), ())), preferred_element_type=F32)


def relay_matrix(experts, chunks):
    size = experts * chunks
    row = lax.broadcasted_iota(jnp.int32, (size, size), 0)
    col = lax.broadcasted_iota(jnp.int32, (size, size), 1)
    wanted = lax.rem(row, chunks) * experts + lax.div(row, chunks)
    return jnp.where(col == wanted, 1.0, 0.0).astype(BF16)


def route_kernel(experts, capacity, ids_ref, gates_ref, tokens_ref, query_ref, out_ref, rest_ref):
    top_count, tok_count = ids_ref.shape
    width = tokens_ref.shape[1]
    chunks = width // LANES
    extra = capacity - GROUP
    expert = lax.broadcasted_iota(jnp.int32, (experts, tok_count), 0)
    member = jnp.zeros((experts, tok_count), F32)
    gate = jnp.zeros((experts, tok_count), F32)
    gates = gates_ref[...].astype(F32)
    for k in range(top_count):
        hit = ids_ref[k : k + 1, :] == expert
        member = member + jnp.where(hit, 1.0, 0.0)
        gate = gate + jnp.where(hit, gates[k : k + 1, :], 0.0)
    earlier = jnp.where(
        lax.broadcasted_iota(jnp.int32, (tok_count, tok_count), 0)
        < lax.broadcasted_iota(jnp.int32, (tok_count, tok_count), 1),
        1.0,
        0.0,
    ).astype(BF16)
    slot = jnp.where(member > 0.0, dot(member.astype(BF16), earlier), -1.0)

    slot_rows = jnp.broadcast_to(slot[:, None, :], (experts, GROUP, tok_count))
    gate_rows = jnp.broadcast_to(gate[:, None, :], (experts, GROUP, tok_count))
    number = lax.broadcasted_iota(jnp.int32, (experts, GROUP, tok_count), 1).astype(F32)
    chosen = slot_rows == number
    rows = experts * GROUP
    place = jnp.where(chosen, 1.0, 0.0).reshape(rows, tok_count).astype(BF16)
    weigh = jnp.where(chosen, gate_rows, 0.0).reshape(rows, tok_count).astype(BF16)
    out_ref[:, :width] = dot(place, tokens_ref[...]).astype(BF16)
    out_ref[:, width : 2 * width] = dot(weigh, query_ref[...]).astype(BF16)

    for i in range(extra):
        chosen = slot == float(GROUP + i)
        place = jnp.where(chosen, 1.0, 0.0).astype(BF16)
        weigh = jnp.where(chosen, gate, 0.0).astype(BF16)
        some_tokens = dot(place, tokens_ref[...]).astype(BF16)
        some_scaled = dot(weigh, query_ref[...]).astype(BF16)
        for c in range(chunks):
            at, cut = slice(c * experts, (c + 1) * experts), slice(c * LANES, (c + 1) * LANES)
            rest_ref[at, i * LANES : (i + 1) * LANES] = some_tokens[:, cut]
            rest_ref[at, (extra + i) * LANES : (extra + i + 1) * LANES] = some_scaled[:, cut]
    out_ref[:, 2 * width :] = dot(relay_matrix(experts, chunks), rest_ref[...]).astype(BF16)


def route(ids, gates, tokens, query, experts, capacity):
    tok_count, width = tokens.shape
    extra = capacity - GROUP
    return pl.pallas_call(
        functools.partial(route_kernel, experts, capacity),
        out_shape=jax.ShapeDtypeStruct((experts * GROUP, 2 * width + 2 * extra * LANES), BF16),
        in_specs=[pl.BlockSpec(memory_space=pltpu.VMEM)] * 4,
        out_specs=pl.BlockSpec(memory_space=pltpu.VMEM),
        scratch_shapes=[pltpu.VMEM((experts * width // LANES, 2 * extra * LANES), BF16)],
        compiler_params=pltpu.CompilerParams(vmem_limit_bytes=32 << 20),
        cost_estimate=pl.CostEstimate(flops=10**9, bytes_accessed=4 * 10**6, transcendentals=0),
    )(ids, gates, tokens, query)


def join_kernel(xs, index_ref, *refs):
    blocks, out_ref = refs[:-1], refs[-1]
    x, core = index_ref[0], index_ref[1]
    for dx in range(xs):
        for dc in range(2):
            source = lax.rem(x + xs - dx, xs) * 2 + lax.rem(core + dc, 2)
            at = pl.ds(pl.multiple_of(source * LANES, LANES), LANES)
            out_ref[:, at] = blocks[dx * 2 + dc][...]


def join(index, blocks, xs):
    rows = blocks[0].shape[0]
    return pl.pallas_call(
        functools.partial(join_kernel, xs),
        out_shape=jax.ShapeDtypeStruct((rows, len(blocks) * LANES), BF16),
        in_specs=[pl.BlockSpec(memory_space=pltpu.SMEM)]
        + [pl.BlockSpec(memory_space=pltpu.VMEM)] * len(blocks),
        out_specs=pl.BlockSpec(memory_space=pltpu.VMEM),
        compiler_params=pltpu.CompilerParams(vmem_limit_bytes=32 << 20),
        cost_estimate=pl.CostEstimate(flops=0, bytes_accessed=6 * 10**6, transcendentals=0),
    )(index, *blocks)


def make_factors(gate_pre, up_pre, error_hidden, tangent):
    sigmoid_a = 1.0 / (1.0 + jnp.exp(-gate_pre))
    slope = sigmoid_a * (1.0 + gate_pre * (1.0 - sigmoid_a))
    bend = sigmoid_a * (1.0 - sigmoid_a) * (2.0 + gate_pre * (1.0 - 2.0 * sigmoid_a))
    both = error_hidden * tangent
    return both * up_pre * bend, both * slope


def expert_kernel(
    experts, extra, xs, index_ref, got_ref, gate_up_ref, down_dir_ref, own_ref, other_ref, rows_ref, scaled_ref, factors_ref
):
    hidden = down_dir_ref.shape[0] // 2
    width = gate_up_ref.shape[1]
    chunks = width // LANES
    main = experts * GROUP
    rows_ref[:main, :] = got_ref[:, :width]
    scaled_ref[:main, :] = got_ref[:, width : 2 * width]
    relay = relay_matrix(experts, chunks)
    rest = dot(relay, got_ref[:, 2 * width :], ((0,), (0,))).astype(BF16)
    for i in range(extra):
        at = slice(main + i * experts, main + (i + 1) * experts)
        for c in range(chunks):
            part, cut = rest[c * experts : (c + 1) * experts], slice(c * LANES, (c + 1) * LANES)
            rows_ref[at, cut] = part[:, i * LANES : (i + 1) * LANES]
            scaled_ref[at, cut] = part[:, (extra + i) * LANES : (extra + i + 1) * LANES]

    step = hidden // 4
    last = ((1,), (1,))

    @pl.loop(0, 4)
    def _(j):
        low = pl.ds(pl.multiple_of(j * step, 16), step)
        high = pl.ds(pl.multiple_of(hidden + j * step, 16), step)
        gate_pre = dot(gate_up_ref[low, :], rows_ref[...], last)
        up_pre = dot(gate_up_ref[high, :], rows_ref[...], last)
        tangent = dot(down_dir_ref[high, :], rows_ref[...], last)
        error = dot(down_dir_ref[low, :], scaled_ref[...], last)
        first, second = make_factors(gate_pre, up_pre, error, tangent)
        factors_ref[low, :] = first.astype(BF16)
        factors_ref[high, :] = second.astype(BF16)

    x, core = index_ref[0], index_ref[1]
    pair = 2 * LANES

    @pl.loop(0, xs)
    def _(d):
        chip = lax.rem(x + d, xs)
        columns = rows_ref[:, pl.ds(pl.multiple_of(chip * pair, pair), pair)]
        for half in range(2):
            at = slice(half * hidden, (half + 1) * hidden)
            product = dot(factors_ref[at, :], columns)
            left, right = product[:, :LANES], product[:, LANES:]
            own_ref[d, at, :] = jnp.where(core == 0, left, right).astype(BF16)
            other_ref[d, at, :] = jnp.where(core == 0, right, left).astype(BF16)


def expert(index, got, gate_up, down_dir, experts, extra, xs):
    width = gate_up.shape[1]
    both = gate_up.shape[0]
    rows = experts * (GROUP + extra)
    part = jax.ShapeDtypeStruct((xs, both, LANES), BF16)
    return pl.pallas_call(
        functools.partial(expert_kernel, experts, extra, xs),
        out_shape=(part, part),
        in_specs=[pl.BlockSpec(memory_space=pltpu.SMEM)] + [pl.BlockSpec(memory_space=pltpu.VMEM)] * 3,
        out_specs=(pl.BlockSpec(memory_space=pltpu.VMEM),) * 2,
        scratch_shapes=[
            pltpu.VMEM((rows, width), BF16),
            pltpu.VMEM((rows, width), BF16),
            pltpu.VMEM((both, rows), BF16),
        ],
        compiler_params=pltpu.CompilerParams(vmem_limit_bytes=48 << 20),
        cost_estimate=pl.CostEstimate(flops=72 * 10**8, bytes_accessed=12 * 10**6, transcendentals=10**6),
    )(index, got, gate_up, down_dir)


def on_device(tokens, query, expert_ids, gate_probs, w_gate_up, w_down, dir_gate):
    experts = lax.axis_size("ep")
    replicas = lax.axis_size("rep")
    xs = replicas // 2
    tok_count, top_count = expert_ids.shape
    width = tokens.shape[1]
    hidden = dir_gate.shape[2]
    capacity = tok_count * top_count // experts + 1
    extra = capacity - GROUP
    me = lax.axis_index("rep")
    index = jnp.stack([me // 2, me % 2]).astype(jnp.int32)

    def shift(dx, dc):
        return [(r, (r // 2 + dx) % xs * 2 + (r + dc) % 2) for r in range(replicas)]

    send = route(expert_ids.T, gate_probs.T, tokens, query, experts, capacity)
    got = lax.all_to_all(
        send.reshape(experts, GROUP, -1), "ep", split_axis=0, concat_axis=0, tiled=True
    ).reshape(experts * GROUP, -1)

    mine = jnp.concatenate([w_down[0].T, dir_gate[0].T], axis=0)
    blocks = [
        lax.ppermute(mine, "rep", shift(dx, dc)) if dx or dc else mine
        for dx in range(xs)
        for dc in range(2)
    ]
    down_dir = join(index, blocks, xs)
    own, other = expert(index, got, w_gate_up[0].T, down_dir, experts, extra, xs)

    f32 = lambda value: value.astype(F32)
    total = f32(own) + f32(lax.ppermute(other, "rep", shift(0, 1)))
    far = total[2].astype(BF16)
    right = lax.ppermute(far[:hidden], "rep", shift(1, 0))
    left = lax.ppermute(far[hidden:], "rep", shift(-1, 0))
    to_right = jnp.concatenate([total[1][:hidden] + f32(right), total[1][hidden:]], axis=0).astype(BF16)
    to_left = jnp.concatenate([total[3][:hidden], total[3][hidden:] + f32(left)], axis=0).astype(BF16)
    result = (
        total[0]
        + f32(lax.ppermute(to_right, "rep", shift(1, 0)))
        + f32(lax.ppermute(to_left, "rep", shift(-1, 0)))
    )
    return result.T[None]


def solution(mesh):
    return jax.shard_map(
        on_device,
        mesh=mesh,
        in_specs=(
            P(("rep", "ep"), None),
            P(("rep", "ep"), None),
            P(("rep", "ep"), None),
            P(("rep", "ep"), None),
            P("ep", None, None),
            P("ep", "rep", None),
            P("ep", "rep", None),
        ),
        out_specs=P("ep", "rep", None),
        check_vma=False,
    )
```

```python
import functools

import jax
import jax.numpy as jnp
from jax import lax
from jax.experimental import pallas as pl
from jax.experimental.pallas import tpu as pltpu
from jax.sharding import PartitionSpec as P

F32 = jnp.float32
BF16 = jnp.bfloat16
LANES = 128
SIDE = 8
GROUP = 8


def dot(a, b, contract=((1,), (0,))):
    return lax.dot_general(a, b, (contract, ((), ())), preferred_element_type=F32)


def dest_of(block):
    return block % SIDE * SIDE + (block // SIDE + block) % SIDE


def relay_matrix(outer, inner):
    size = outer * inner
    row = lax.broadcasted_iota(jnp.int32, (size, size), 0)
    col = lax.broadcasted_iota(jnp.int32, (size, size), 1)
    wanted = (row & (inner - 1)) * outer + (row >> (inner.bit_length() - 1))
    return jnp.where(col == wanted, 1.0, 0.0).astype(BF16)


def route_kernel(
    experts, capacity, ids_hbm, gates_hbm, tokens_hbm, query_hbm, out_hbm, ids_ref, gates_ref, tokens_ref, query_ref, rest_ref, out_ref, sems
):
    top_count, tok_count = ids_ref.shape
    width = tokens_ref.shape[1]
    chunks = width // LANES
    extra = capacity - GROUP
    pairs = ((ids_hbm, ids_ref), (gates_hbm, gates_ref), (tokens_hbm, tokens_ref), (query_hbm, query_ref))
    loads = [pltpu.make_async_copy(source, target, sems.at[i]) for i, (source, target) in enumerate(pairs)]
    for load in loads:
        load.start()
    edges = (0, width, 2 * width, out_ref.shape[1])
    stores = [
        pltpu.make_async_copy(out_ref.at[:, low:high], out_hbm.at[:, low:high], sems.at[4 + i])
        for i, (low, high) in enumerate(zip(edges[:-1], edges[1:]))
    ]
    earlier = jnp.where(
        lax.broadcasted_iota(jnp.int32, (tok_count, tok_count), 0)
        < lax.broadcasted_iota(jnp.int32, (tok_count, tok_count), 1),
        1.0,
        0.0,
    ).astype(BF16)
    block = lax.broadcasted_iota(jnp.int32, (experts, tok_count), 0)
    expert = dest_of(block)
    member = jnp.zeros((experts, tok_count), F32)
    gate = jnp.zeros((experts, tok_count), F32)
    loads[0].wait()
    loads[1].wait()
    gates = gates_ref[...].astype(F32)
    for k in range(top_count):
        hit = ids_ref[k : k + 1, :] == expert
        member = member + jnp.where(hit, 1.0, 0.0)
        gate = gate + jnp.where(hit, gates[k : k + 1, :], 0.0)
    slot = jnp.where(member > 0.0, dot(member.astype(BF16), earlier), -1.0)

    slot_rows = jnp.broadcast_to(slot[:, None, :], (experts, GROUP, tok_count))
    gate_rows = jnp.broadcast_to(gate[:, None, :], (experts, GROUP, tok_count))
    number = lax.broadcasted_iota(jnp.int32, (experts, GROUP, tok_count), 1).astype(F32)
    chosen = slot_rows == number
    rows = experts * GROUP
    place = jnp.where(chosen, 1.0, 0.0).reshape(rows, tok_count).astype(BF16)
    weigh = jnp.where(chosen, gate_rows, 0.0).reshape(rows, tok_count).astype(BF16)
    loads[2].wait()
    out_ref[:, :width] = dot(place, tokens_ref[...]).astype(BF16)
    stores[0].start()
    loads[3].wait()
    out_ref[:, width : 2 * width] = dot(weigh, query_ref[...]).astype(BF16)
    stores[1].start()

    for i in range(extra):
        chosen = slot == float(GROUP + i)
        place = jnp.where(chosen, 1.0, 0.0).astype(BF16)
        weigh = jnp.where(chosen, gate, 0.0).astype(BF16)
        some_tokens = dot(place, tokens_ref[...]).astype(BF16)
        some_scaled = dot(weigh, query_ref[...]).astype(BF16)
        for c in range(chunks):
            at, cut = slice(c * experts, (c + 1) * experts), slice(c * LANES, (c + 1) * LANES)
            rest_ref[at, i * LANES : (i + 1) * LANES] = some_tokens[:, cut]
            rest_ref[at, (extra + i) * LANES : (extra + i + 1) * LANES] = some_scaled[:, cut]
    out_ref[:, 2 * width :] = dot(relay_matrix(experts, chunks), rest_ref[...]).astype(BF16)
    stores[2].start()
    for store in stores:
        store.wait()


def route(ids, gates, tokens, query, experts, capacity):
    width = tokens.shape[1]
    extra = capacity - GROUP
    out = (experts * GROUP, 2 * width + 2 * extra * LANES)
    return pl.pallas_call(
        functools.partial(route_kernel, experts, capacity),
        out_shape=jax.ShapeDtypeStruct(out, BF16),
        in_specs=[pl.BlockSpec(memory_space=pltpu.HBM)] * 4,
        out_specs=pl.BlockSpec(memory_space=pltpu.HBM),
        scratch_shapes=[pltpu.VMEM(v.shape, v.dtype) for v in (ids, gates, tokens, query)]
        + [
            pltpu.VMEM((experts * width // LANES, 2 * extra * LANES), BF16),
            pltpu.VMEM(out, BF16),
            pltpu.SemaphoreType.DMA((7,)),
        ],
        compiler_params=pltpu.CompilerParams(vmem_limit_bytes=32 << 20),
        cost_estimate=pl.CostEstimate(flops=10**9, bytes_accessed=4 * 10**6, transcendentals=0),
    )(*(pltpu.with_memory_space_constraint(value, pltpu.HBM) for value in (ids, gates, tokens, query)))


def join_kernel(xs, index_ref, *refs):
    blocks, out_ref = refs[:-1], refs[-1]
    x, core = index_ref[0], index_ref[1]
    for dx in range(xs):
        for dc in range(2):
            source = lax.rem(x + xs - dx, xs) * 2 + lax.rem(core + dc, 2)
            at = pl.ds(pl.multiple_of(source * LANES, LANES), LANES)
            out_ref[:, at] = blocks[dx * 2 + dc][...]


def join(index, blocks, xs):
    rows = blocks[0].shape[0]
    return pl.pallas_call(
        functools.partial(join_kernel, xs),
        out_shape=jax.ShapeDtypeStruct((rows, len(blocks) * LANES), BF16),
        in_specs=[pl.BlockSpec(memory_space=pltpu.SMEM)]
        + [pl.BlockSpec(memory_space=pltpu.VMEM)] * len(blocks),
        out_specs=pl.BlockSpec(memory_space=pltpu.VMEM),
        compiler_params=pltpu.CompilerParams(vmem_limit_bytes=32 << 20),
        cost_estimate=pl.CostEstimate(flops=0, bytes_accessed=6 * 10**6, transcendentals=0),
    )(index, *blocks)


def make_factors(gate_pre, up_pre, error_hidden, tangent):
    sigmoid_a = 1.0 / (1.0 + jnp.exp(-gate_pre))
    slope = sigmoid_a * (1.0 + gate_pre * (1.0 - sigmoid_a))
    bend = sigmoid_a * (1.0 - sigmoid_a) * (2.0 + gate_pre * (1.0 - 2.0 * sigmoid_a))
    both = error_hidden * tangent
    return both * up_pre * bend, both * slope


def slot_of(d, core):
    return jnp.where(d == 0, 3, jnp.where(d == 2, 0, jnp.where((d == 1) == (core == 0), 2, 1)))


def expert_kernel(
    experts,
    extra,
    xs,
    index_ref,
    got_ref,
    gate_up_hbm,
    down_dir_hbm,
    own_ref,
    first_ref,
    other_ref,
    rows_ref,
    scaled_ref,
    factors_ref,
    gate_up_ref,
    down_dir_ref,
    sems,
):
    loads = [
        pltpu.make_async_copy(gate_up_hbm, gate_up_ref, sems.at[0]),
        pltpu.make_async_copy(down_dir_hbm, down_dir_ref, sems.at[1]),
    ]
    for load in loads:
        load.start()
    hidden = down_dir_ref.shape[0] // 2
    width = gate_up_ref.shape[1]
    chunks = width // LANES
    main = experts * GROUP
    rows_ref[:main, :] = got_ref[:, :width]
    scaled_ref[:main, :] = got_ref[:, width : 2 * width]
    rest = dot(relay_matrix(chunks, experts), got_ref[:, 2 * width :]).astype(BF16)
    for i in range(extra):
        at = slice(main + i * experts, main + (i + 1) * experts)
        for c in range(chunks):
            part, cut = rest[c * experts : (c + 1) * experts], slice(c * LANES, (c + 1) * LANES)
            rows_ref[at, cut] = part[:, i * LANES : (i + 1) * LANES]
            scaled_ref[at, cut] = part[:, (extra + i) * LANES : (extra + i + 1) * LANES]

    last = ((1,), (1,))
    loads[0].wait()
    gate_pre = dot(gate_up_ref[:hidden, :], rows_ref[...], last)
    up_pre = dot(gate_up_ref[hidden:, :], rows_ref[...], last)
    loads[1].wait()
    tangent = dot(down_dir_ref[hidden:, :], rows_ref[...], last)
    error = dot(down_dir_ref[:hidden, :], scaled_ref[...], last)
    first, second = make_factors(gate_pre, up_pre, error, tangent)
    factors_ref[:hidden, :] = first.astype(BF16)
    factors_ref[hidden:, :] = second.astype(BF16)

    x, core = index_ref[0], index_ref[1]
    pair = 2 * LANES

    for half in range(2):
        at = slice(half * hidden, (half + 1) * hidden)
        product = dot(factors_ref[at, :], rows_ref[...])
        for chip in range(xs):
            ahead = (chip - x) & (xs - 1)
            left = product[:, chip * pair : chip * pair + LANES]
            right = product[:, chip * pair + LANES : (chip + 1) * pair]
            own_ref[slot_of(ahead, core), at, :] = jnp.where(core == 0, left, right).astype(BF16)
            others = jnp.where(core == 0, right, left).astype(BF16)
            slot = slot_of(ahead, 1 - core)

            @pl.when(slot < 2)
            def _():
                first_ref[slot, at, :] = others

            @pl.when(slot >= 2)
            def _():
                other_ref[slot - 2, at, :] = others


def expert(index, got, gate_up, down_dir, experts, extra, xs):
    width = gate_up.shape[1]
    both = gate_up.shape[0]
    rows = experts * (GROUP + extra)
    outs = [jax.ShapeDtypeStruct(shape + (both, LANES), BF16) for shape in ((xs,), (2,), (xs - 2,))]
    return pl.pallas_call(
        functools.partial(expert_kernel, experts, extra, xs),
        out_shape=outs,
        in_specs=[
            pl.BlockSpec(memory_space=pltpu.SMEM),
            pl.BlockSpec(memory_space=pltpu.VMEM),
            pl.BlockSpec(memory_space=pltpu.HBM),
            pl.BlockSpec(memory_space=pltpu.HBM),
        ],
        out_specs=[pl.BlockSpec(memory_space=pltpu.VMEM)] * 3,
        scratch_shapes=[
            pltpu.VMEM((rows, width), BF16),
            pltpu.VMEM((rows, width), BF16),
            pltpu.VMEM((both, rows), BF16),
            pltpu.VMEM(gate_up.shape, BF16),
            pltpu.VMEM(down_dir.shape, BF16),
            pltpu.SemaphoreType.DMA((2,)),
        ],
        compiler_params=pltpu.CompilerParams(vmem_limit_bytes=36 << 20),
        cost_estimate=pl.CostEstimate(flops=72 * 10**8, bytes_accessed=12 * 10**6, transcendentals=10**6),
    )(index, got, *(pltpu.with_memory_space_constraint(value, pltpu.HBM) for value in (gate_up, down_dir)))


def finish_kernel(own_ref, other_ref, near_ref, last_ref, out_ref):
    home = own_ref[own_ref.shape[0] - 1].astype(F32) + other_ref[other_ref.shape[0] - 1].astype(F32)
    out_ref[...] = (home + near_ref[...].astype(F32) + last_ref[...].astype(F32)).T


def finish(own, other, near, last):
    both, lanes = last.shape
    return pl.pallas_call(
        finish_kernel,
        out_shape=jax.ShapeDtypeStruct((lanes, both), F32),
        in_specs=[pl.BlockSpec(memory_space=pltpu.VMEM)] * 4,
        out_specs=pl.BlockSpec(memory_space=pltpu.VMEM),
        compiler_params=pltpu.CompilerParams(vmem_limit_bytes=16 << 20),
        cost_estimate=pl.CostEstimate(flops=10**6, bytes_accessed=3 * 10**6, transcendentals=0),
    )(own, other, near, last)


def on_device(tokens, query, expert_ids, gate_probs, w_gate_up, w_down, dir_gate):
    experts = lax.axis_size("ep")
    replicas = lax.axis_size("rep")
    xs = replicas // 2
    tok_count, top_count = expert_ids.shape
    width = tokens.shape[1]
    hidden = dir_gate.shape[2]
    capacity = tok_count * top_count // experts + 1
    extra = capacity - GROUP
    me = lax.axis_index("rep")
    index = jnp.stack([me // 2, me % 2]).astype(jnp.int32)

    def shift(dx, dc):
        return [(r, (r // 2 + dx) % xs * 2 + (r + dc) % 2) for r in range(replicas)]

    send = route(expert_ids.T, gate_probs.T, tokens, query, experts, capacity)
    got = lax.all_to_all(
        send.reshape(experts, GROUP, -1),
        "ep",
        split_axis=0,
        concat_axis=0,
        tiled=True,
        axis_index_groups=[[dest_of(block) for block in range(experts)]],
    ).reshape(experts * GROUP, -1)

    mine = jnp.concatenate([w_down[0].T, dir_gate[0].T], axis=0)
    blocks = [
        lax.ppermute(mine, "rep", shift(dx, dc)) if dx or dc else mine
        for dx in range(xs)
        for dc in range(2)
    ]
    down_dir = join(index, blocks, xs)
    own, first, other = expert(index, got, w_gate_up[0].T, down_dir, experts, extra, xs)

    f32 = lambda value: value.astype(F32)
    onward = [(r, (r // 2 + (1 if r % 2 == 0 else -1)) % xs * 2 + r % 2) for r in range(replicas)]
    back = [(to, r) for r, to in onward]
    first = lax.ppermute(first, "rep", shift(0, 1))
    other = lax.ppermute(other, "rep", shift(0, 1))
    passed = lax.ppermute((f32(own[0]) + f32(first[0])).astype(BF16), "rep", onward)
    near = lax.ppermute((f32(own[1]) + f32(first[1])).astype(BF16), "rep", back)
    passed, near = lax.optimization_barrier((passed, near))
    joined = (f32(own[2]) + f32(other[0]) + f32(passed)).astype(BF16)
    return finish(own, other, near, lax.ppermute(joined, "rep", onward))[None]


def solution(mesh):
    return jax.shard_map(
        on_device,
        mesh=mesh,
        in_specs=(
            P(("rep", "ep"), None),
            P(("rep", "ep"), None),
            P(("rep", "ep"), None),
            P(("rep", "ep"), None),
            P("ep", None, None),
            P("ep", "rep", None),
            P("ep", "rep", None),
        ),
        out_specs=P("ep", "rep", None),
        check_vma=False,
    )
```

```python
import functools

import jax
import jax.numpy as jnp
from jax import lax
from jax.experimental import pallas as pl
from jax.experimental.pallas import tpu as pltpu
from jax.sharding import PartitionSpec as P

F32 = jnp.float32
BF16 = jnp.bfloat16
LANES = 128
SIDE = 8
GROUP = 8


def dot(a, b, contract=((1,), (0,))):
    return lax.dot_general(a, b, (contract, ((), ())), preferred_element_type=F32)


def place_of(index_ref):
    return index_ref[0] >> 1, index_ref[0] & 1


def dest_of(block, core):
    return block % SIDE * SIDE + (block // SIDE + SIDE // 2 * core + block) % SIDE


def relay_matrix(outer, inner):
    size = outer * inner
    row = lax.broadcasted_iota(jnp.int32, (size, size), 0)
    col = lax.broadcasted_iota(jnp.int32, (size, size), 1)
    wanted = (row & (inner - 1)) * outer + (row >> (inner.bit_length() - 1))
    return jnp.where(col == wanted, 1.0, 0.0).astype(BF16)


def route_kernel(
    experts, capacity, index_ref, ids_hbm, gates_hbm, tokens_hbm, query_hbm, out_hbm, ids_ref, gates_ref, tokens_ref, query_ref, rest_ref, out_ref, sems
):
    top_count, tok_count = ids_ref.shape
    width = tokens_ref.shape[1]
    chunks = width // LANES
    extra = capacity - GROUP
    pairs = ((ids_hbm, ids_ref), (gates_hbm, gates_ref), (tokens_hbm, tokens_ref), (query_hbm, query_ref))
    loads = [pltpu.make_async_copy(source, target, sems.at[i]) for i, (source, target) in enumerate(pairs)]
    for load in loads:
        load.start()
    edges = (0, width, 2 * width, out_ref.shape[1])
    stores = [
        pltpu.make_async_copy(out_ref.at[:, low:high], out_hbm.at[:, low:high], sems.at[4 + i])
        for i, (low, high) in enumerate(zip(edges[:-1], edges[1:]))
    ]
    earlier = jnp.where(
        lax.broadcasted_iota(jnp.int32, (tok_count, tok_count), 0)
        < lax.broadcasted_iota(jnp.int32, (tok_count, tok_count), 1),
        1.0,
        0.0,
    ).astype(BF16)
    block = lax.broadcasted_iota(jnp.int32, (experts, tok_count), 0)
    _, core = place_of(index_ref)
    expert = dest_of(block, core)
    member = jnp.zeros((experts, tok_count), F32)
    gate = jnp.zeros((experts, tok_count), F32)
    loads[0].wait()
    loads[1].wait()
    gates = gates_ref[...].astype(F32)
    for k in range(top_count):
        hit = ids_ref[k : k + 1, :] == expert
        member = member + jnp.where(hit, 1.0, 0.0)
        gate = gate + jnp.where(hit, gates[k : k + 1, :], 0.0)
    slot = jnp.where(member > 0.0, dot(member.astype(BF16), earlier), -1.0)

    slot_rows = jnp.broadcast_to(slot[:, None, :], (experts, GROUP, tok_count))
    gate_rows = jnp.broadcast_to(gate[:, None, :], (experts, GROUP, tok_count))
    number = lax.broadcasted_iota(jnp.int32, (experts, GROUP, tok_count), 1).astype(F32)
    chosen = slot_rows == number
    rows = experts * GROUP
    place = jnp.where(chosen, 1.0, 0.0).reshape(rows, tok_count).astype(BF16)
    weigh = jnp.where(chosen, gate_rows, 0.0).reshape(rows, tok_count).astype(BF16)
    loads[2].wait()
    out_ref[:, :width] = dot(place, tokens_ref[...]).astype(BF16)
    stores[0].start()
    loads[3].wait()
    out_ref[:, width : 2 * width] = dot(weigh, query_ref[...]).astype(BF16)
    stores[1].start()

    for i in range(extra):
        chosen = slot == float(GROUP + i)
        place = jnp.where(chosen, 1.0, 0.0).astype(BF16)
        weigh = jnp.where(chosen, gate, 0.0).astype(BF16)
        some_tokens = dot(place, tokens_ref[...]).astype(BF16)
        some_scaled = dot(weigh, query_ref[...]).astype(BF16)
        for c in range(chunks):
            at, cut = slice(c * experts, (c + 1) * experts), slice(c * LANES, (c + 1) * LANES)
            rest_ref[at, i * LANES : (i + 1) * LANES] = some_tokens[:, cut]
            rest_ref[at, (extra + i) * LANES : (extra + i + 1) * LANES] = some_scaled[:, cut]
    out_ref[:, 2 * width :] = dot(relay_matrix(experts, chunks), rest_ref[...]).astype(BF16)
    stores[2].start()
    for store in stores:
        store.wait()


def route(index, ids, gates, tokens, query, experts, capacity):
    width = tokens.shape[1]
    extra = capacity - GROUP
    out = (experts * GROUP, 2 * width + 2 * extra * LANES)
    return pl.pallas_call(
        functools.partial(route_kernel, experts, capacity),
        out_shape=jax.ShapeDtypeStruct(out, BF16),
        in_specs=[pl.BlockSpec(memory_space=pltpu.SMEM)] + [pl.BlockSpec(memory_space=pltpu.HBM)] * 4,
        out_specs=pl.BlockSpec(memory_space=pltpu.HBM),
        scratch_shapes=[pltpu.VMEM(v.shape, v.dtype) for v in (ids, gates, tokens, query)]
        + [
            pltpu.VMEM((experts * width // LANES, 2 * extra * LANES), BF16),
            pltpu.VMEM(out, BF16),
            pltpu.SemaphoreType.DMA((7,)),
        ],
        compiler_params=pltpu.CompilerParams(vmem_limit_bytes=32 << 20),
        cost_estimate=pl.CostEstimate(flops=10**9, bytes_accessed=4 * 10**6, transcendentals=0),
    )(index, *(pltpu.with_memory_space_constraint(value, pltpu.HBM) for value in (ids, gates, tokens, query)))


def join_kernel(xs, index_ref, *refs):
    blocks, out_ref = refs[:-1], refs[-1]
    x, core = place_of(index_ref)
    for dx in range(xs):
        for dc in range(2):
            source = lax.rem(x + xs - dx, xs) * 2 + lax.rem(core + dc, 2)
            at = pl.ds(pl.multiple_of(source * LANES, LANES), LANES)
            out_ref[:, at] = blocks[dx * 2 + dc][...]


def join(index, blocks, xs):
    rows = blocks[0].shape[0]
    return pl.pallas_call(
        functools.partial(join_kernel, xs),
        out_shape=jax.ShapeDtypeStruct((rows, len(blocks) * LANES), BF16),
        in_specs=[pl.BlockSpec(memory_space=pltpu.SMEM)]
        + [pl.BlockSpec(memory_space=pltpu.VMEM)] * len(blocks),
        out_specs=pl.BlockSpec(memory_space=pltpu.VMEM),
        compiler_params=pltpu.CompilerParams(vmem_limit_bytes=32 << 20),
        cost_estimate=pl.CostEstimate(flops=0, bytes_accessed=6 * 10**6, transcendentals=0),
    )(index, *blocks)


def make_factors(gate_pre, up_pre, error_hidden, tangent):
    sigmoid_a = 1.0 / (1.0 + jnp.exp(-gate_pre))
    slope = sigmoid_a * (1.0 + gate_pre * (1.0 - sigmoid_a))
    bend = sigmoid_a * (1.0 - sigmoid_a) * (2.0 + gate_pre * (1.0 - 2.0 * sigmoid_a))
    both = error_hidden * tangent
    return both * up_pre * bend, both * slope


def ahead_of(slot, core):
    if slot in (0, 3):
        return 2 if slot == 0 else 0
    return jnp.where((core == 0) == (slot == 1), 3, 1)


def put_products(slots, xs, index_ref, rows_ref, factors_ref, own_ref, other_ref):
    x, core = place_of(index_ref)
    for place, slot in enumerate(slots):
        columns = []
        for home in (core, 1 - core):
            start = ((x + ahead_of(slot, home)) & (xs - 1)) * 2 * LANES + home * LANES
            columns.append(rows_ref[:, pl.ds(pl.multiple_of(start, LANES), LANES)])
        product = dot(factors_ref[...], jnp.concatenate(columns, axis=1))
        own_ref[place] = product[:, :LANES].astype(BF16)
        other_ref[place] = product[:, LANES:].astype(BF16)


def expert_kernel(
    experts,
    extra,
    xs,
    index_ref,
    got_ref,
    gate_up_hbm,
    down_dir_hbm,
    own_ref,
    first_ref,
    rows_ref,
    factors_ref,
    scaled_ref,
    gate_up_ref,
    down_dir_ref,
    sems,
):
    loads = [
        pltpu.make_async_copy(gate_up_hbm, gate_up_ref, sems.at[0]),
        pltpu.make_async_copy(down_dir_hbm, down_dir_ref, sems.at[1]),
    ]
    for load in loads:
        load.start()
    hidden = down_dir_ref.shape[0] // 2
    width = gate_up_ref.shape[1]
    chunks = width // LANES
    main = experts * GROUP
    rows_ref[:main, :] = got_ref[:, :width]
    scaled_ref[:main, :] = got_ref[:, width : 2 * width]
    rest = dot(relay_matrix(chunks, experts), got_ref[:, 2 * width :]).astype(BF16)
    for i in range(extra):
        at = slice(main + i * experts, main + (i + 1) * experts)
        for c in range(chunks):
            part, cut = rest[c * experts : (c + 1) * experts], slice(c * LANES, (c + 1) * LANES)
            rows_ref[at, cut] = part[:, i * LANES : (i + 1) * LANES]
            scaled_ref[at, cut] = part[:, (extra + i) * LANES : (extra + i + 1) * LANES]

    last = ((1,), (1,))
    loads[0].wait()
    gate_pre = dot(gate_up_ref[:hidden, :], rows_ref[...], last)
    up_pre = dot(gate_up_ref[hidden:, :], rows_ref[...], last)
    loads[1].wait()
    tangent = dot(down_dir_ref[hidden:, :], rows_ref[...], last)
    error = dot(down_dir_ref[:hidden, :], scaled_ref[...], last)
    first, second = make_factors(gate_pre, up_pre, error, tangent)
    factors_ref[:hidden, :] = first.astype(BF16)
    factors_ref[hidden:, :] = second.astype(BF16)

    put_products((0, 1), xs, index_ref, rows_ref, factors_ref, own_ref, first_ref)


def home_products_kernel(xs, index_ref, rows_ref, factors_ref, home_ref, other_ref):
    put_products((2, 3), xs, index_ref, rows_ref, factors_ref, home_ref, other_ref)


def home_products(index, rows, factors, xs):
    part = jax.ShapeDtypeStruct((2, factors.shape[0], LANES), BF16)
    return pl.pallas_call(
        functools.partial(home_products_kernel, xs),
        out_shape=[part] * 2,
        in_specs=[pl.BlockSpec(memory_space=pltpu.SMEM)] + [pl.BlockSpec(memory_space=pltpu.VMEM)] * 2,
        out_specs=[pl.BlockSpec(memory_space=pltpu.VMEM)] * 2,
        compiler_params=pltpu.CompilerParams(vmem_limit_bytes=24 << 20),
        cost_estimate=pl.CostEstimate(flops=12 * 10**8, bytes_accessed=5 * 10**6, transcendentals=0),
    )(index, rows, factors)


def expert(index, got, gate_up, down_dir, experts, extra, xs):
    width = gate_up.shape[1]
    both = gate_up.shape[0]
    rows = experts * (GROUP + extra)
    part = jax.ShapeDtypeStruct((2, both, LANES), BF16)
    outs = [part, part, jax.ShapeDtypeStruct((rows, width), BF16), jax.ShapeDtypeStruct((both, rows), BF16)]
    return pl.pallas_call(
        functools.partial(expert_kernel, experts, extra, xs),
        out_shape=outs,
        in_specs=[
            pl.BlockSpec(memory_space=pltpu.SMEM),
            pl.BlockSpec(memory_space=pltpu.VMEM),
            pl.BlockSpec(memory_space=pltpu.HBM),
            pl.BlockSpec(memory_space=pltpu.HBM),
        ],
        out_specs=[pl.BlockSpec(memory_space=pltpu.VMEM)] * 4,
        scratch_shapes=[
            pltpu.VMEM((rows, width), BF16),
            pltpu.VMEM(gate_up.shape, BF16),
            pltpu.VMEM(down_dir.shape, BF16),
            pltpu.SemaphoreType.DMA((2,)),
        ],
        compiler_params=pltpu.CompilerParams(vmem_limit_bytes=36 << 20),
        cost_estimate=pl.CostEstimate(flops=72 * 10**8, bytes_accessed=12 * 10**6, transcendentals=10**6),
    )(index, got, *(pltpu.with_memory_space_constraint(value, pltpu.HBM) for value in (gate_up, down_dir)))


def home_kernel(own_ref, other_ref, near_ref, out_ref):
    home = own_ref[own_ref.shape[0] - 1].astype(F32) + other_ref[other_ref.shape[0] - 1].astype(F32)
    out_ref[...] = (home + near_ref[...].astype(F32)).T


def finish_kernel(home_ref, last_ref, out_ref):
    out_ref[...] = home_ref[...] + last_ref[...].astype(F32).T


def turned(kernel, *operands):
    both, lanes = operands[-1].shape
    return pl.pallas_call(
        kernel,
        out_shape=jax.ShapeDtypeStruct((lanes, both), F32),
        in_specs=[pl.BlockSpec(memory_space=pltpu.VMEM)] * len(operands),
        out_specs=pl.BlockSpec(memory_space=pltpu.VMEM),
        compiler_params=pltpu.CompilerParams(vmem_limit_bytes=16 << 20),
        cost_estimate=pl.CostEstimate(flops=10**6, bytes_accessed=3 * 10**6, transcendentals=0),
    )(*operands)


def on_device(tokens, query, expert_ids, gate_probs, w_gate_up, w_down, dir_gate):
    experts = lax.axis_size("ep")
    replicas = lax.axis_size("rep")
    xs = replicas // 2
    tok_count, top_count = expert_ids.shape
    width = tokens.shape[1]
    hidden = dir_gate.shape[2]
    capacity = tok_count * top_count // experts + 1
    extra = capacity - GROUP
    me = lax.axis_index("rep")
    index = me.astype(jnp.int32).reshape(1)

    def shift(dx, dc):
        return [(r, (r // 2 + dx) % xs * 2 + (r + dc) % 2) for r in range(replicas)]

    send = route(index, expert_ids.T, gate_probs.T, tokens, query, experts, capacity)
    got = lax.all_to_all(
        send.reshape(experts, GROUP, -1),
        ("rep", "ep"),
        split_axis=0,
        concat_axis=0,
        tiled=True,
        axis_index_groups=[
            [r * experts + dest_of(block, r % 2) for block in range(experts)] for r in range(replicas)
        ],
    ).reshape(experts * GROUP, -1)

    mine = jnp.concatenate([w_down[0].T, dir_gate[0].T], axis=0)
    blocks = [
        lax.ppermute(mine, "rep", shift(dx, dc)) if dx or dc else mine
        for dx in range(xs)
        for dc in range(2)
    ]
    down_dir = join(index, blocks, xs)
    own, first, rows, factors = expert(index, got, w_gate_up[0].T, down_dir, experts, extra, xs)

    f32 = lambda value: value.astype(F32)
    onward = [(r, (r // 2 + (1 if r % 2 == 0 else -1)) % xs * 2 + r % 2) for r in range(replicas)]
    back = [(to, r) for r, to in onward]
    home, other = home_products(index, rows, factors, xs)
    first = lax.ppermute(first, "rep", shift(0, 1))
    other = lax.ppermute(other, "rep", shift(0, 1))
    passed = lax.ppermute((f32(own[0]) + f32(first[0])).astype(BF16), "rep", onward)
    near = lax.ppermute((f32(own[1]) + f32(first[1])).astype(BF16), "rep", back)
    joined = (f32(home[0]) + f32(other[0]) + f32(passed)).astype(BF16)
    last = lax.ppermute(joined, "rep", onward)
    return turned(finish_kernel, turned(home_kernel, home, other, near), last)[None]


def solution(mesh):
    return jax.shard_map(
        on_device,
        mesh=mesh,
        in_specs=(
            P(("rep", "ep"), None),
            P(("rep", "ep"), None),
            P(("rep", "ep"), None),
            P(("rep", "ep"), None),
            P("ep", None, None),
            P("ep", "rep", None),
            P("ep", "rep", None),
        ),
        out_specs=P("ep", "rep", None),
        check_vma=False,
    )
```

```python
import functools

import jax
import jax.numpy as jnp
from jax import lax
from jax.experimental import pallas as pl
from jax.experimental.pallas import tpu as pltpu
from jax.sharding import PartitionSpec as P

F32 = jnp.float32
BF16 = jnp.bfloat16
LANES = 128
SIDE = 8
GROUP = 8


def dot(a, b, contract=((1,), (0,))):
    return lax.dot_general(a, b, (contract, ((), ())), preferred_element_type=F32)


def place_of(index_ref):
    return index_ref[0] >> 1, index_ref[0] & 1


def dest_of(block, core):
    return block % SIDE * SIDE + (block // SIDE + SIDE // 2 * core + block) % SIDE


def relay_matrix(outer, inner):
    size = outer * inner
    row = lax.broadcasted_iota(jnp.int32, (size, size), 0)
    col = lax.broadcasted_iota(jnp.int32, (size, size), 1)
    wanted = (row & (inner - 1)) * outer + (row >> (inner.bit_length() - 1))
    return jnp.where(col == wanted, 1.0, 0.0).astype(BF16)


def route_kernel(
    experts, capacity, index_ref, ids_hbm, gates_hbm, tokens_hbm, query_hbm, out_hbm, ids_ref, gates_ref, tokens_ref, query_ref, rest_ref, out_ref, sems
):
    top_count, tok_count = ids_ref.shape
    width = tokens_ref.shape[1]
    chunks = width // LANES
    extra = capacity - GROUP
    pairs = ((ids_hbm, ids_ref), (gates_hbm, gates_ref), (tokens_hbm, tokens_ref), (query_hbm, query_ref))
    loads = [pltpu.make_async_copy(source, target, sems.at[i]) for i, (source, target) in enumerate(pairs)]
    for load in loads:
        load.start()
    edges = (0, width, 2 * width, out_ref.shape[1])
    stores = [
        pltpu.make_async_copy(out_ref.at[:, low:high], out_hbm.at[:, low:high], sems.at[4 + i])
        for i, (low, high) in enumerate(zip(edges[:-1], edges[1:]))
    ]
    earlier = jnp.where(
        lax.broadcasted_iota(jnp.int32, (tok_count, tok_count), 0)
        < lax.broadcasted_iota(jnp.int32, (tok_count, tok_count), 1),
        1.0,
        0.0,
    ).astype(BF16)
    block = lax.broadcasted_iota(jnp.int32, (experts, tok_count), 0)
    _, core = place_of(index_ref)
    expert = dest_of(block, core)
    member = jnp.zeros((experts, tok_count), F32)
    gate = jnp.zeros((experts, tok_count), F32)
    loads[0].wait()
    loads[1].wait()
    gates = gates_ref[...].astype(F32)
    for k in range(top_count):
        hit = ids_ref[k : k + 1, :] == expert
        member = member + jnp.where(hit, 1.0, 0.0)
        gate = gate + jnp.where(hit, gates[k : k + 1, :], 0.0)
    slot = jnp.where(member > 0.0, dot(member.astype(BF16), earlier), -1.0)

    slot_rows = jnp.broadcast_to(slot[:, None, :], (experts, GROUP, tok_count))
    gate_rows = jnp.broadcast_to(gate[:, None, :], (experts, GROUP, tok_count))
    number = lax.broadcasted_iota(jnp.int32, (experts, GROUP, tok_count), 1).astype(F32)
    chosen = slot_rows == number
    rows = experts * GROUP
    place = jnp.where(chosen, 1.0, 0.0).reshape(rows, tok_count).astype(BF16)
    weigh = jnp.where(chosen, gate_rows, 0.0).reshape(rows, tok_count).astype(BF16)
    loads[2].wait()
    out_ref[:, :width] = dot(place, tokens_ref[...]).astype(BF16)
    stores[0].start()
    loads[3].wait()
    out_ref[:, width : 2 * width] = dot(weigh, query_ref[...]).astype(BF16)
    stores[1].start()

    for i in range(extra):
        chosen = slot == float(GROUP + i)
        place = jnp.where(chosen, 1.0, 0.0).astype(BF16)
        weigh = jnp.where(chosen, gate, 0.0).astype(BF16)
        some_tokens = dot(place, tokens_ref[...]).astype(BF16)
        some_scaled = dot(weigh, query_ref[...]).astype(BF16)
        for c in range(chunks):
            at, cut = slice(c * experts, (c + 1) * experts), slice(c * LANES, (c + 1) * LANES)
            rest_ref[at, i * LANES : (i + 1) * LANES] = some_tokens[:, cut]
            rest_ref[at, (extra + i) * LANES : (extra + i + 1) * LANES] = some_scaled[:, cut]
    out_ref[:, 2 * width :] = dot(relay_matrix(experts, chunks), rest_ref[...]).astype(BF16)
    stores[2].start()
    for store in stores:
        store.wait()


def route(index, ids, gates, tokens, query, experts, capacity):
    width = tokens.shape[1]
    extra = capacity - GROUP
    out = (experts * GROUP, 2 * width + 2 * extra * LANES)
    return pl.pallas_call(
        functools.partial(route_kernel, experts, capacity),
        out_shape=jax.ShapeDtypeStruct(out, BF16),
        in_specs=[pl.BlockSpec(memory_space=pltpu.SMEM)] + [pl.BlockSpec(memory_space=pltpu.HBM)] * 4,
        out_specs=pl.BlockSpec(memory_space=pltpu.HBM),
        scratch_shapes=[pltpu.VMEM(v.shape, v.dtype) for v in (ids, gates, tokens, query)]
        + [
            pltpu.VMEM((experts * width // LANES, 2 * extra * LANES), BF16),
            pltpu.VMEM(out, BF16),
            pltpu.SemaphoreType.DMA((7,)),
        ],
        compiler_params=pltpu.CompilerParams(vmem_limit_bytes=32 << 20),
        cost_estimate=pl.CostEstimate(flops=10**9, bytes_accessed=4 * 10**6, transcendentals=0),
    )(index, *(pltpu.with_memory_space_constraint(value, pltpu.HBM) for value in (ids, gates, tokens, query)))


def join_kernel(xs, index_ref, *refs):
    blocks, out_ref = refs[:-1], refs[-1]
    x, core = place_of(index_ref)
    for dx in range(xs):
        for dc in range(2):
            source = lax.rem(x + xs - dx, xs) * 2 + lax.rem(core + dc, 2)
            at = pl.ds(pl.multiple_of(source * LANES, LANES), LANES)
            out_ref[:, at] = blocks[dx * 2 + dc][...]


def join(index, blocks, xs):
    rows = blocks[0].shape[0]
    return pl.pallas_call(
        functools.partial(join_kernel, xs),
        out_shape=jax.ShapeDtypeStruct((rows, len(blocks) * LANES), BF16),
        in_specs=[pl.BlockSpec(memory_space=pltpu.SMEM)]
        + [pl.BlockSpec(memory_space=pltpu.VMEM)] * len(blocks),
        out_specs=pl.BlockSpec(memory_space=pltpu.VMEM),
        compiler_params=pltpu.CompilerParams(vmem_limit_bytes=32 << 20),
        cost_estimate=pl.CostEstimate(flops=0, bytes_accessed=6 * 10**6, transcendentals=0),
    )(index, *blocks)


def make_factors(gate_pre, up_pre, error_hidden, tangent):
    sigmoid_a = 1.0 / (1.0 + jnp.exp(-gate_pre))
    slope = sigmoid_a * (1.0 + gate_pre * (1.0 - sigmoid_a))
    bend = sigmoid_a * (1.0 - sigmoid_a) * (2.0 + gate_pre * (1.0 - 2.0 * sigmoid_a))
    both = error_hidden * tangent
    return both * up_pre * bend, both * slope


def ahead_of(slot, core):
    if slot in (0, 3):
        return 2 if slot == 0 else 0
    return jnp.where((core == 0) == (slot == 1), 3, 1)


def put_products(slots, xs, index_ref, rows_ref, factors_ref, own_ref, other_ref):
    x, core = place_of(index_ref)
    for place, slot in enumerate(slots):
        columns = []
        for home in (core, 1 - core):
            start = ((x + ahead_of(slot, home)) & (xs - 1)) * 2 * LANES + home * LANES
            columns.append(rows_ref[:, pl.ds(pl.multiple_of(start, LANES), LANES)])
        product = dot(factors_ref[...], jnp.concatenate(columns, axis=1))
        own_ref[place] = product[:, :LANES].astype(BF16)
        other_ref[place] = product[:, LANES:].astype(BF16)


def expert_kernel(
    experts,
    extra,
    xs,
    index_ref,
    got_ref,
    gate_up_hbm,
    down_dir_hbm,
    own_ref,
    first_ref,
    rows_ref,
    factors_ref,
    scaled_ref,
    gate_up_ref,
    down_dir_ref,
    sems,
):
    loads = [
        pltpu.make_async_copy(gate_up_hbm, gate_up_ref, sems.at[0]),
        pltpu.make_async_copy(down_dir_hbm, down_dir_ref, sems.at[1]),
    ]
    for load in loads:
        load.start()
    hidden = down_dir_ref.shape[0] // 2
    width = gate_up_ref.shape[1]
    chunks = width // LANES
    main = experts * GROUP
    rows_ref[:main, :] = got_ref[:, :width]
    scaled_ref[:main, :] = got_ref[:, width : 2 * width]
    rest = dot(relay_matrix(chunks, experts), got_ref[:, 2 * width :]).astype(BF16)
    for i in range(extra):
        at = slice(main + i * experts, main + (i + 1) * experts)
        for c in range(chunks):
            part, cut = rest[c * experts : (c + 1) * experts], slice(c * LANES, (c + 1) * LANES)
            rows_ref[at, cut] = part[:, i * LANES : (i + 1) * LANES]
            scaled_ref[at, cut] = part[:, (extra + i) * LANES : (extra + i + 1) * LANES]

    last = ((1,), (1,))
    loads[0].wait()
    gate_pre = dot(gate_up_ref[:hidden, :], rows_ref[...], last)
    up_pre = dot(gate_up_ref[hidden:, :], rows_ref[...], last)
    loads[1].wait()
    tangent = dot(down_dir_ref[hidden:, :], rows_ref[...], last)
    error = dot(down_dir_ref[:hidden, :], scaled_ref[...], last)
    first, second = make_factors(gate_pre, up_pre, error, tangent)
    factors_ref[:hidden, :] = first.astype(BF16)
    factors_ref[hidden:, :] = second.astype(BF16)

    put_products((0, 1), xs, index_ref, rows_ref, factors_ref, own_ref, first_ref)


def home_products_kernel(xs, index_ref, rows_ref, factors_ref, home_ref, other_ref):
    put_products((2, 3), xs, index_ref, rows_ref, factors_ref, home_ref, other_ref)


def home_products(index, rows, factors, xs):
    part = jax.ShapeDtypeStruct((2, factors.shape[0], LANES), BF16)
    return pl.pallas_call(
        functools.partial(home_products_kernel, xs),
        out_shape=[part] * 2,
        in_specs=[pl.BlockSpec(memory_space=pltpu.SMEM)] + [pl.BlockSpec(memory_space=pltpu.VMEM)] * 2,
        out_specs=[pl.BlockSpec(memory_space=pltpu.VMEM)] * 2,
        compiler_params=pltpu.CompilerParams(vmem_limit_bytes=24 << 20),
        cost_estimate=pl.CostEstimate(flops=12 * 10**8, bytes_accessed=5 * 10**6, transcendentals=0),
    )(index, rows, factors)


def expert(index, got, gate_up, down_dir, experts, extra, xs):
    width = gate_up.shape[1]
    both = gate_up.shape[0]
    rows = experts * (GROUP + extra)
    part = jax.ShapeDtypeStruct((2, both, LANES), BF16)
    outs = [part, part, jax.ShapeDtypeStruct((rows, width), BF16), jax.ShapeDtypeStruct((both, rows), BF16)]
    return pl.pallas_call(
        functools.partial(expert_kernel, experts, extra, xs),
        out_shape=outs,
        in_specs=[
            pl.BlockSpec(memory_space=pltpu.SMEM),
            pl.BlockSpec(memory_space=pltpu.VMEM),
            pl.BlockSpec(memory_space=pltpu.HBM),
            pl.BlockSpec(memory_space=pltpu.HBM),
        ],
        out_specs=[pl.BlockSpec(memory_space=pltpu.VMEM)] * 4,
        scratch_shapes=[
            pltpu.VMEM((rows, width), BF16),
            pltpu.VMEM(gate_up.shape, BF16),
            pltpu.VMEM(down_dir.shape, BF16),
            pltpu.SemaphoreType.DMA((2,)),
        ],
        compiler_params=pltpu.CompilerParams(vmem_limit_bytes=36 << 20),
        cost_estimate=pl.CostEstimate(flops=72 * 10**8, bytes_accessed=12 * 10**6, transcendentals=10**6),
    )(index, got, *(pltpu.with_memory_space_constraint(value, pltpu.HBM) for value in (gate_up, down_dir)))


def home_kernel(own_ref, other_ref, near_ref, out_ref):
    home = own_ref[own_ref.shape[0] - 1].astype(F32) + other_ref[other_ref.shape[0] - 1].astype(F32)
    out_ref[...] = (home + near_ref[...].astype(F32)).T


def finish_kernel(home_ref, last_ref, out_ref):
    out_ref[...] = home_ref[...] + last_ref[...].astype(F32).T


def turned(kernel, *operands):
    both, lanes = operands[-1].shape
    return pl.pallas_call(
        kernel,
        out_shape=jax.ShapeDtypeStruct((lanes, both), F32),
        in_specs=[pl.BlockSpec(memory_space=pltpu.VMEM)] * len(operands),
        out_specs=pl.BlockSpec(memory_space=pltpu.VMEM),
        compiler_params=pltpu.CompilerParams(vmem_limit_bytes=16 << 20),
        cost_estimate=pl.CostEstimate(flops=10**6, bytes_accessed=3 * 10**6, transcendentals=0),
    )(*operands)


def on_device(tokens, query, expert_ids, gate_probs, w_gate_up, w_down, dir_gate):
    experts = lax.axis_size("ep")
    replicas = lax.axis_size("rep")
    xs = replicas // 2
    tok_count, top_count = expert_ids.shape
    width = tokens.shape[1]
    hidden = dir_gate.shape[2]
    capacity = tok_count * top_count // experts + 1
    extra = capacity - GROUP
    me = lax.axis_index("rep")
    index = me.astype(jnp.int32).reshape(1)

    def shift(dx, dc):
        return [(r, (r // 2 + dx) % xs * 2 + (r + dc) % 2) for r in range(replicas)]

    send = route(index, expert_ids.T, gate_probs.T, tokens, query, experts, capacity)
    got = lax.all_to_all(
        send.reshape(experts, GROUP, -1),
        ("rep", "ep"),
        split_axis=0,
        concat_axis=0,
        tiled=True,
        axis_index_groups=[
            [r * experts + dest_of(block, r % 2) for block in range(experts)] for r in range(replicas)
        ],
    ).reshape(experts * GROUP, -1)

    mine = jnp.concatenate([w_down[0].T, dir_gate[0].T], axis=0)
    near_blocks = [mine] + [lax.ppermute(mine, "rep", shift(dx, 0)) for dx in range(1, xs)]
    swapped = lax.ppermute(jnp.concatenate(near_blocks, axis=0), "rep", shift(0, 1))
    both = 2 * hidden
    blocks = [
        block for dx in range(xs) for block in (near_blocks[dx], swapped[dx * both : (dx + 1) * both])
    ]
    down_dir = join(index, blocks, xs)
    own, first, rows, factors = expert(index, got, w_gate_up[0].T, down_dir, experts, extra, xs)

    f32 = lambda value: value.astype(F32)
    onward = [(r, (r // 2 + (1 if r % 2 == 0 else -1)) % xs * 2 + r % 2) for r in range(replicas)]
    back = [(to, r) for r, to in onward]
    home, other = home_products(index, rows, factors, xs)
    first = lax.ppermute(first, "rep", shift(0, 1))
    other = lax.ppermute(other, "rep", shift(0, 1))
    passed = lax.ppermute((f32(own[0]) + f32(first[0])).astype(BF16), "rep", onward)
    near = lax.ppermute((f32(own[1]) + f32(first[1])).astype(BF16), "rep", back)
    joined = (f32(home[0]) + f32(other[0]) + f32(passed)).astype(BF16)
    last = lax.ppermute(joined, "rep", onward)
    return turned(finish_kernel, turned(home_kernel, home, other, near), last)[None]


def solution(mesh):
    return jax.shard_map(
        on_device,
        mesh=mesh,
        in_specs=(
            P(("rep", "ep"), None),
            P(("rep", "ep"), None),
            P(("rep", "ep"), None),
            P(("rep", "ep"), None),
            P("ep", None, None),
            P("ep", "rep", None),
            P("ep", "rep", None),
        ),
        out_specs=P("ep", "rep", None),
        check_vma=False,
    )
```
